32 devices in a mesh: boxes: 32 (over z, y, x, core).
Axes of the slice: x: 2, y: 2, z: 4, core: 2. Of those that a mesh axis runs over, the one named last changes fastest.
Arguments:
- random_block: bfloat16 [512, 256, 128], P('boxes'), may hold values from -6 to 6
- sample_block: bfloat16 [512, 256, 128], P('boxes'), may hold values from -12 to 12
- near_blocks: bfloat16 [512, 8, 256, 256], P('boxes'), may hold values from -0.375 to 0.375
- near_index: int32 [512, 8], P('boxes'), may hold values from 0 to 511, as said below
- near_count: int32 [512], P('boxes'), may hold values from 2 to 8
Outputs:
- leaf_sketch: bfloat16 [512, 256, 128], P('boxes')
- level_sketch: bfloat16 [32, 9, 128, 128], P('boxes')
The draws below stay inside these ranges and needn't reach their ends.
Inputs may be any that keep to these rules, and one draw needn't show every extreme that they name: near_index[b, 0] = b; every entry lies within 16 boxes of b; entries at slots from near_count[b] on are ignored.
All inputs are finite; a program needn't handle non-finite values.
Results may differ from the reference program's by a relative error of at most 0.001.
Values may be sent and summed in bfloat16 or wider, within the bound.
A program may use at most 192 MiB of HBM per device.

```python
import jax
import jax.numpy as jnp
from jax import lax

LEAF = 256
RANK = 64
SAMPLES = 128
MAXNEAR = 8
BOX_DEV = 16
NBOX = 512
LEVELS = 9
N_BOXES = 32


def draw_near_count(key, part):
    heavy_flag = jax.random.randint(jax.random.fold_in(key, 12), (NBOX // BOX_DEV,), 0, 2)
    heavy_rows = jnp.repeat(heavy_flag, BOX_DEV)
    light_draw = jax.random.randint(jax.random.fold_in(key, 13), (NBOX,), 2, MAXNEAR // 2 + 1)
    heavy_draw = jax.random.randint(jax.random.fold_in(key, 14), (NBOX,), MAXNEAR // 2 + 1, MAXNEAR + 1)
    counts = jnp.where(heavy_rows == 1, heavy_draw, light_draw)
    return counts.at[0].set(MAXNEAR).astype(jnp.int32)


def draw_near_index(key, part):
    boxes_ids = jnp.arange(NBOX)
    offsets = jax.random.randint(jax.random.fold_in(key, 21), (NBOX, MAXNEAR), -BOX_DEV, BOX_DEV + 1)
    sign_pick = jax.random.randint(jax.random.fold_in(key, 22), (NBOX,), 0, 2) * 2 - 1
    offsets = offsets.at[:, 0].set(0).at[:, 1].set(sign_pick * BOX_DEV)
    return jnp.clip(boxes_ids[:, None] + offsets, 0, NBOX - 1).astype(jnp.int32)


def steps_of(stream_key, extent, pieces, smallest, top_value):
    level, own = 1.0, jax.random.fold_in(stream_key, 6)
    for position, parts in pieces:
        draws = jnp.exp(jax.random.uniform(jax.random.fold_in(own, position), (parts,), jnp.float32, smallest / len(pieces), top_value / len(pieces)))
        level = level * jnp.repeat(draws, extent[position] // parts).reshape([-1 if axis == position else 1 for axis in range(len(extent))])
    return level


def scatter_about(rng, dims, scale, most, cuts=(), dtype=jnp.bfloat16):
    gain = steps_of(rng, dims, cuts, -0.22, 0.18) if cuts else 1.0
    array = jax.random.normal(rng, dims, jnp.float32) * scale * gain
    return jnp.minimum(jnp.maximum(array, -most), most).astype(dtype)


def setup_inputs(seed: int = 0) -> dict:
    arg_keys = jax.random.split(jax.random.key(seed), 6)
    return {
        "random_block": scatter_about(arg_keys[0], (NBOX, LEAF, SAMPLES), 1.0, 6.0, ((0, 32),)),
        "sample_block": scatter_about(arg_keys[1], (NBOX, LEAF, SAMPLES), 2.0, 12.0, ((0, 32),)),
        "near_blocks": scatter_about(arg_keys[2], (NBOX, MAXNEAR, LEAF, LEAF), LEAF ** -0.5, 0.375, ((0, 32),)),
        "near_index": draw_near_index(jax.random.fold_in(arg_keys[5], 71), 0),
        "near_count": draw_near_count(jax.random.fold_in(arg_keys[5], 71), 0),
    }


exact_mode = lax.Precision.HIGHEST

def lower_solve(factor, compact):
    return jax.scipy.linalg.solve_triangular(factor, compact.T, lower=True)

def basis_step(sample, random):
    compact = sample[:, :, :RANK] + sample[:, :, RANK:]
    gram = jnp.einsum('bik,bil->bkl', compact, compact, precision=exact_mode)
    factor = jnp.linalg.cholesky(gram)
    rows_q = jax.vmap(lower_solve)(factor, compact)
    reduced = jnp.einsum('bki,bis->bks', rows_q, sample, precision=exact_mode)
    projected = jnp.einsum('bki,bis->bks', rows_q, random, precision=exact_mode)
    sketch = jnp.einsum('bki,bks->bis', rows_q, projected, precision=exact_mode)
    return (reduced, projected, sketch)

def reference(random_block, sample_block, near_blocks, near_index, near_count):
    slots = jnp.arange(MAXNEAR)

    def near_term(packed):
        blocks, indices, length = packed
        picked = jnp.take(random_block, indices, axis=0).astype(jnp.float32)
        keep_mask = (slots < length).astype(jnp.float32)
        picked = picked * keep_mask[:, None, None]
        return jnp.einsum('mij,mjs->is', blocks.astype(jnp.float32), picked)
    near_sum = lax.map(near_term, (near_blocks, near_index, near_count))
    far_sample = sample_block.astype(jnp.float32) - near_sum
    reduced, projected, sketch = basis_step(far_sample, random_block.astype(jnp.float32))
    leaf_sketch = sketch.astype(jnp.bfloat16)
    firsts = jnp.arange(N_BOXES) * BOX_DEV
    records = []
    nodes = NBOX
    for height in range(LEVELS):
        nodes = nodes // 2
        reduced, projected, sketch = basis_step(reduced.reshape(nodes, 2 * RANK, SAMPLES), projected.reshape(nodes, 2 * RANK, SAMPLES))
        records.append(jnp.take(sketch, firsts // 2 ** (height + 1), axis=0))
    level_sketch = jnp.stack(records, axis=1).astype(jnp.bfloat16)
    return (leaf_sketch, level_sketch)
```

```python
import functools

import jax
import jax.numpy as jnp
from jax import lax
from jax.experimental import pallas as pl
from jax.experimental.pallas import tpu as pltpu
from jax.sharding import PartitionSpec as P

exact_mode = lax.Precision.HIGHEST


def exact_dot(a, b):
    return jnp.dot(a, b, precision=exact_mode, preferred_element_type=jnp.float32)


def gram_kernel(ids, counts, blocks, sample, low, own, high, grams, compact, wide, sems):
    box = pl.program_id(0)
    count = own.shape[0]
    slots, samples = blocks.shape[1], sample.shape[2]
    half = samples // 2

    @pl.when(box == 0)
    def _():
        copies = [
            pltpu.make_async_copy(part, wide.at[pl.ds(place * count, count)], sems.at[place])
            for place, part in enumerate((low, own, high))
        ]
        for copy in copies:
            copy.start()
        for copy in copies:
            copy.wait()

    total = jnp.zeros(sample.shape[1:], jnp.float32)
    for slot in range(slots):
        keep = (slot < counts[box]).astype(jnp.float32).astype(jnp.bfloat16)
        picked = wide[ids[box * slots + slot]] * keep
        total += jnp.dot(blocks[0, slot], picked, preferred_element_type=jnp.float32)
    far = sample[0].astype(jnp.float32) - total
    doubled = far + pltpu.roll(far, half, 1)
    compact[0] = doubled
    random = wide[count + box].astype(jnp.float32)
    flipped = doubled.T[:half]
    grams[0] = exact_dot(flipped, jnp.concatenate([doubled, random], axis=1))


def gram_call(ids, counts, blocks, sample, low, own, high):
    count, rows, samples = sample.shape
    slots = blocks.shape[1]
    half = samples // 2
    anywhere = pl.BlockSpec(memory_space=pl.ANY)
    return pl.pallas_call(
        gram_kernel,
        grid_spec=pltpu.PrefetchScalarGridSpec(
            num_scalar_prefetch=2,
            grid=(count,),
            in_specs=[
                pl.BlockSpec((1, slots, rows, rows), lambda b, *_: (b, 0, 0, 0)),
                pl.BlockSpec((1, rows, samples), lambda b, *_: (b, 0, 0)),
                anywhere,
                anywhere,
                anywhere,
            ],
            out_specs=[
                pl.BlockSpec((1, half, 2 * samples), lambda b, *_: (b, 0, 0)),
                pl.BlockSpec((1, rows, samples), lambda b, *_: (b, 0, 0)),
            ],
            scratch_shapes=[
                pltpu.VMEM((3 * count, rows, samples), jnp.bfloat16),
                pltpu.SemaphoreType.DMA((3,)),
            ],
        ),
        out_shape=[
            jax.ShapeDtypeStruct((count, half, 2 * samples), jnp.float32),
            jax.ShapeDtypeStruct((count, rows, samples), jnp.float32),
        ],
        name="gram",
    )(ids, counts, blocks, sample, low, own, high)


def eliminate(total, half, work, uppers, with_upper):
    samples = 2 * half
    lanes = lax.broadcasted_iota(jnp.int32, (1, samples), 1)

    def step(k, carry):
        at_k = lanes == k
        for node in range(total):
            matrix = work[node]
            row = work[node, pl.ds(k, 1), :]
            column = jnp.sum(jnp.where(at_k, matrix, 0.0), axis=1, keepdims=True)
            pivot = jnp.sum(jnp.where(at_k, row, 0.0), axis=1, keepdims=True)
            scaled = row / pivot
            work[node] = matrix - column * scaled
            work[node, pl.ds(k, 1), :] = scaled
            if node in with_upper:
                kept = (lanes >= k) & (lanes < half)
                uppers[with_upper[node], pl.ds(k, 1), :] = jnp.where(
                    kept, row * lax.rsqrt(pivot), 0.0
                )
        return carry

    lax.fori_loop(0, half, step, 0)


def start_matrix(gram, half):
    samples = 2 * half
    rows = lax.broadcasted_iota(jnp.int32, (half, samples), 0)
    lanes = lax.broadcasted_iota(jnp.int32, (half, samples), 1)
    return jnp.where(lanes < half, gram, (lanes - half == rows).astype(jnp.float32))


def solved(work, node, moment):
    blank = jnp.zeros_like(moment)
    answer = exact_dot(work[node], jnp.concatenate([blank, moment], axis=0))
    return jnp.concatenate([answer, blank], axis=0)


def local_kernel(grams, compact, leaf_out, level_out, work, moments, uppers):
    count = grams.shape[0]
    half, samples = grams.shape[1], grams.shape[2] // 2
    depth = count.bit_length() - 1
    total = work.shape[0]
    for node in range(count):
        work[node] = start_matrix(grams[node, :, :samples], half)
    spans = []
    for height in range(1, depth + 1):
        spans += [(0, 2**height)] if height == depth else [(0, 2**height), (2**height, 2 ** (height + 1))]
    for place, (first, last) in enumerate(spans):
        summed = grams[first]
        for leaf in range(first + 1, last):
            summed = summed + grams[leaf]
        work[count + place] = start_matrix(summed[:, :samples], half)
        moments[place] = summed[:, samples:]
    with_upper = {0: 0, 1: 1}
    for height in range(1, depth):
        for side in range(2):
            with_upper[count + 2 * (height - 1) + side] = 2 * height + side
    eliminate(total, half, work, uppers, with_upper)
    for leaf in range(count):
        answer = solved(work, leaf, grams[leaf, :, samples:])
        leaf_out[leaf] = exact_dot(compact[leaf], answer).astype(leaf_out.dtype)
    for height in range(1, depth + 1):
        place = 2 * (height - 1)
        answer = solved(work, count + place, moments[place])
        stacked = jnp.concatenate([uppers[place], uppers[place + 1]], axis=0)
        level_out[height - 1] = exact_dot(stacked, answer).astype(level_out.dtype)


def local_call(grams, compact):
    count, half, double = grams.shape
    samples = double // 2
    depth = count.bit_length() - 1
    extra = 2 * depth - 1
    return pl.pallas_call(
        local_kernel,
        out_shape=[
            jax.ShapeDtypeStruct(compact.shape, jnp.bfloat16),
            jax.ShapeDtypeStruct((depth, samples, samples), jnp.bfloat16),
        ],
        scratch_shapes=[
            pltpu.VMEM((count + extra, half, samples), jnp.float32),
            pltpu.VMEM((extra, half, samples), jnp.float32),
            pltpu.VMEM((2 * depth, half, samples), jnp.float32),
        ],
        cost_estimate=pl.CostEstimate(
            flops=500_000_000, bytes_accessed=4_000_000, transcendentals=0
        ),
        name="local",
    )(grams, compact)


def upper_kernel(nodes, level_out, work, uppers):
    total = nodes.shape[0]
    half, samples = nodes.shape[1], nodes.shape[2] // 2
    for node in range(total):
        work[node] = start_matrix(nodes[node, :, :samples], half)
    eliminate(total, half, work, uppers, {node: node for node in range(total - 1)})


def upper_solve(nodes, picks, level_out, work, uppers):
    upper_kernel(nodes, level_out, work, uppers)
    total = nodes.shape[0]
    samples = nodes.shape[2] // 2
    spread = (total - 1) // 2
    for height in range(spread):
        if height == spread - 1:
            answer = solved(work, total - 1, nodes[total - 1, :, samples:])
        else:
            mine = picks[height + 1]
            place = 2 * (height + 1) + mine
            answer = solved(work, place, nodes[place, :, samples:])
        stacked = jnp.concatenate([uppers[2 * height], uppers[2 * height + 1]], axis=0)
        level_out[height] = exact_dot(stacked, answer).astype(level_out.dtype)


def upper_call(nodes, picks):
    total, half, double = nodes.shape
    samples = double // 2
    spread = (total - 1) // 2
    return pl.pallas_call(
        upper_solve,
        in_specs=[
            pl.BlockSpec(memory_space=pltpu.VMEM),
            pl.BlockSpec(memory_space=pltpu.SMEM),
        ],
        out_shape=jax.ShapeDtypeStruct((spread, samples, samples), jnp.bfloat16),
        scratch_shapes=[
            pltpu.VMEM((total, half, samples), jnp.float32),
            pltpu.VMEM((total - 1, half, samples), jnp.float32),
        ],
        name="upper",
    )(nodes, picks)


def per_device(random_block, sample_block, near_blocks, near_index, near_count):
    count = random_block.shape[0]
    device = lax.axis_index("boxes")
    size = lax.axis_size("boxes")
    forward = [(i, i + 1) for i in range(size - 1)]
    backward = [(target, source) for source, target in forward]
    low = lax.ppermute(random_block, "boxes", forward)
    high = lax.ppermute(random_block, "boxes", backward)
    ids = jnp.clip(near_index - device * count + count, 0, 3 * count - 1).reshape(-1)
    grams, compact = gram_call(
        ids, near_count, near_blocks, sample_block, low, random_block, high
    )
    summed = jnp.sum(grams, axis=0)
    nodes = []
    spread = size.bit_length() - 1
    bits = (device >> jnp.arange(spread)) & 1
    for step in range(spread):
        other = lax.ppermute(summed, "boxes", [(i, i ^ (1 << step)) for i in range(size)])
        odd = bits[step] == 1
        nodes += [jnp.where(odd, other, summed), jnp.where(odd, summed, other)]
        summed = summed + other
    nodes.append(summed)
    leaf_sketch, level_low = local_call(grams, compact)
    level_high = upper_call(jnp.stack(nodes), bits.astype(jnp.int32))
    return (leaf_sketch, jnp.concatenate([level_low, level_high], axis=0)[None])


def solution(mesh):
    return jax.shard_map(
        per_device,
        mesh=mesh,
        in_specs=(
            P("boxes", None, None),
            P("boxes", None, None),
            P("boxes", None, None, None),
            P("boxes", None),
            P("boxes"),
        ),
        out_specs=(P("boxes", None, None), P("boxes", None, None, None)),
        check_vma=False,
    )
```

```python
import functools

import jax
import jax.numpy as jnp
from jax import lax
from jax.experimental import pallas as pl
from jax.experimental.pallas import tpu as pltpu
from jax.sharding import PartitionSpec as P

exact_mode = lax.Precision.HIGHEST


def exact_dot(a, b):
    return jnp.dot(a, b, precision=exact_mode, preferred_element_type=jnp.float32)


def gram_kernel(ids, counts, blocks, sample, low, own, high, grams, compact, wide, sems):
    box = pl.program_id(0)
    count = own.shape[0]
    slots, samples = blocks.shape[1], sample.shape[2]
    half = samples // 2

    @pl.when(box == 0)
    def _():
        copies = [
            pltpu.make_async_copy(part, wide.at[pl.ds(place * count, count)], sems.at[place])
            for place, part in enumerate((low, own, high))
        ]
        for copy in copies:
            copy.start()
        for copy in copies:
            copy.wait()

    for part in range(blocks.shape[0]):
        here = box * blocks.shape[0] + part
        total = jnp.zeros(sample.shape[1:], jnp.float32)
        for slot in range(slots):
            keep = (slot < counts[here]).astype(jnp.float32).astype(jnp.bfloat16)
            picked = wide[ids[here * slots + slot]] * keep
            total += jnp.dot(blocks[part, slot], picked, preferred_element_type=jnp.float32)
        far = sample[part].astype(jnp.float32) - total
        doubled = far + pltpu.roll(far, half, 1)
        compact[part] = doubled
        random = wide[count + here].astype(jnp.float32)
        flipped = doubled.T[:half]
        grams[part] = exact_dot(flipped, jnp.concatenate([doubled, random], axis=1))


def gram_call(ids, counts, blocks, sample, low, own, high):
    count, rows, samples = sample.shape
    slots = blocks.shape[1]
    half = samples // 2
    together = 2 if count % 2 == 0 else 1
    anywhere = pl.BlockSpec(memory_space=pl.ANY)
    return pl.pallas_call(
        gram_kernel,
        grid_spec=pltpu.PrefetchScalarGridSpec(
            num_scalar_prefetch=2,
            grid=(count // together,),
            in_specs=[
                pl.BlockSpec((together, slots, rows, rows), lambda b, *_: (b, 0, 0, 0)),
                pl.BlockSpec((together, rows, samples), lambda b, *_: (b, 0, 0)),
                anywhere,
                anywhere,
                anywhere,
            ],
            out_specs=[
                pl.BlockSpec((together, half, 2 * samples), lambda b, *_: (b, 0, 0)),
                pl.BlockSpec((together, rows, samples), lambda b, *_: (b, 0, 0)),
            ],
            scratch_shapes=[
                pltpu.VMEM((3 * count, rows, samples), jnp.bfloat16),
                pltpu.SemaphoreType.DMA((3,)),
            ],
        ),
        out_shape=[
            jax.ShapeDtypeStruct((count, half, 2 * samples), jnp.float32),
            jax.ShapeDtypeStruct((count, rows, samples), jnp.float32),
        ],
        name="gram",
    )(ids, counts, blocks, sample, low, own, high)


def eliminate(total, half, work, uppers, with_upper):
    samples = 2 * half
    lanes = lax.broadcasted_iota(jnp.int32, (1, samples), 1)

    rows = lax.broadcasted_iota(jnp.int32, (half, samples), 0)
    group = 4

    def step(k, carry):
        at_k = lanes == k
        kept = (lanes >= k) & (lanes < half)
        row_k = rows == k
        pivots = [work[node, pl.ds(k, 1), :] for node in range(total)]
        picked = [
            jnp.sum(jnp.where(at_k, row, 0.0), axis=1, keepdims=True) for row in pivots
        ]
        scaled = [row / pivot for row, pivot in zip(pivots, picked)]
        for node, place in with_upper.items():
            uppers[place, pl.ds(k, 1), :] = jnp.where(
                kept, pivots[node] * lax.rsqrt(picked[node]), 0.0
            )
        for first in range(0, total, group):
            members = range(first, min(first + group, total))
            matrices = [work[node] for node in members]
            columns = [
                jnp.sum(jnp.where(at_k, matrix, 0.0), axis=1, keepdims=True)
                for matrix in matrices
            ]
            for node, matrix, column in zip(members, matrices, columns):
                work[node] = jnp.where(row_k, scaled[node], matrix - column * scaled[node])
        return carry

    lax.fori_loop(0, half, step, 0)


def start_matrix(gram, half):
    samples = 2 * half
    rows = lax.broadcasted_iota(jnp.int32, (half, samples), 0)
    lanes = lax.broadcasted_iota(jnp.int32, (half, samples), 1)
    return jnp.where(lanes < half, gram, (lanes - half == rows).astype(jnp.float32))


def solved(work, node, moment):
    blank = jnp.zeros_like(moment)
    answer = exact_dot(work[node], jnp.concatenate([blank, moment], axis=0))
    return jnp.concatenate([answer, blank], axis=0)


def local_kernel(grams, compact, leaf_out, level_out, work, moments, uppers):
    count = grams.shape[0]
    half, samples = grams.shape[1], grams.shape[2] // 2
    depth = count.bit_length() - 1
    total = work.shape[0]
    for node in range(count):
        work[node] = start_matrix(grams[node, :, :samples], half)
    spans = []
    for height in range(1, depth + 1):
        spans += [(0, 2**height)] if height == depth else [(0, 2**height), (2**height, 2 ** (height + 1))]
    for place, (first, last) in enumerate(spans):
        summed = grams[first]
        for leaf in range(first + 1, last):
            summed = summed + grams[leaf]
        work[count + place] = start_matrix(summed[:, :samples], half)
        moments[place] = summed[:, samples:]
    with_upper = {0: 0, 1: 1}
    for height in range(1, depth):
        for side in range(2):
            with_upper[count + 2 * (height - 1) + side] = 2 * height + side
    eliminate(total, half, work, uppers, with_upper)
    for leaf in range(count):
        answer = solved(work, leaf, grams[leaf, :, samples:])
        leaf_out[leaf] = exact_dot(compact[leaf], answer).astype(leaf_out.dtype)
    for height in range(1, depth + 1):
        place = 2 * (height - 1)
        answer = solved(work, count + place, moments[place])
        stacked = jnp.concatenate([uppers[place], uppers[place + 1]], axis=0)
        level_out[height - 1] = exact_dot(stacked, answer).astype(level_out.dtype)


def local_call(grams, compact):
    count, half, double = grams.shape
    samples = double // 2
    depth = count.bit_length() - 1
    extra = 2 * depth - 1
    return pl.pallas_call(
        local_kernel,
        out_shape=[
            jax.ShapeDtypeStruct(compact.shape, jnp.bfloat16),
            jax.ShapeDtypeStruct((depth, samples, samples), jnp.bfloat16),
        ],
        scratch_shapes=[
            pltpu.VMEM((count + extra, half, samples), jnp.float32),
            pltpu.VMEM((extra, half, samples), jnp.float32),
            pltpu.VMEM((2 * depth, half, samples), jnp.float32),
        ],
        cost_estimate=pl.CostEstimate(
            flops=500_000_000, bytes_accessed=4_000_000, transcendentals=0
        ),
        name="local",
    )(grams, compact)


def upper_kernel(nodes, level_out, work, uppers):
    total = nodes.shape[0]
    half, samples = nodes.shape[1], nodes.shape[2] // 2
    for node in range(total):
        work[node] = start_matrix(nodes[node, :, :samples], half)
    eliminate(total, half, work, uppers, {node: node for node in range(total - 1)})


def upper_solve(nodes, picks, level_out, work, uppers):
    upper_kernel(nodes, level_out, work, uppers)
    total = nodes.shape[0]
    samples = nodes.shape[2] // 2
    spread = (total - 1) // 2
    for height in range(spread):
        if height == spread - 1:
            answer = solved(work, total - 1, nodes[total - 1, :, samples:])
        else:
            mine = picks[height + 1]
            place = 2 * (height + 1) + mine
            answer = solved(work, place, nodes[place, :, samples:])
        stacked = jnp.concatenate([uppers[2 * height], uppers[2 * height + 1]], axis=0)
        level_out[height] = exact_dot(stacked, answer).astype(level_out.dtype)


def upper_call(nodes, picks):
    total, half, double = nodes.shape
    samples = double // 2
    spread = (total - 1) // 2
    return pl.pallas_call(
        upper_solve,
        in_specs=[
            pl.BlockSpec(memory_space=pltpu.VMEM),
            pl.BlockSpec(memory_space=pltpu.SMEM),
        ],
        out_shape=jax.ShapeDtypeStruct((spread, samples, samples), jnp.bfloat16),
        scratch_shapes=[
            pltpu.VMEM((total, half, samples), jnp.float32),
            pltpu.VMEM((total - 1, half, samples), jnp.float32),
        ],
        name="upper",
    )(nodes, picks)


def per_device(random_block, sample_block, near_blocks, near_index, near_count):
    count = random_block.shape[0]
    device = lax.axis_index("boxes")
    size = lax.axis_size("boxes")
    forward = [(i, i + 1) for i in range(size - 1)]
    backward = [(target, source) for source, target in forward]
    low = lax.ppermute(random_block, "boxes", forward)
    high = lax.ppermute(random_block, "boxes", backward)
    ids = jnp.clip(near_index - device * count + count, 0, 3 * count - 1).reshape(-1)
    grams, compact = gram_call(
        ids, near_count, near_blocks, sample_block, low, random_block, high
    )
    summed = jnp.sum(grams, axis=0)
    nodes = []
    spread = size.bit_length() - 1
    bits = (device >> jnp.arange(spread)) & 1
    for step in range(spread):
        other = lax.ppermute(summed, "boxes", [(i, i ^ (1 << step)) for i in range(size)])
        odd = bits[step] == 1
        nodes += [jnp.where(odd, other, summed), jnp.where(odd, summed, other)]
        summed = summed + other
    nodes.append(summed)
    leaf_sketch, level_low = local_call(grams, compact)
    level_high = upper_call(jnp.stack(nodes), bits.astype(jnp.int32))
    return (leaf_sketch, jnp.concatenate([level_low, level_high], axis=0)[None])


def solution(mesh):
    return jax.shard_map(
        per_device,
        mesh=mesh,
        in_specs=(
            P("boxes", None, None),
            P("boxes", None, None),
            P("boxes", None, None, None),
            P("boxes", None),
            P("boxes"),
        ),
        out_specs=(P("boxes", None, None), P("boxes", None, None, None)),
        check_vma=False,
    )
```

```python
import functools

import jax
import jax.numpy as jnp
from jax import lax
from jax.experimental import pallas as pl
from jax.experimental.pallas import tpu as pltpu
from jax.sharding import PartitionSpec as P

exact_mode = lax.Precision.HIGHEST


def exact_dot(a, b):
    return jnp.dot(a, b, precision=exact_mode, preferred_element_type=jnp.float32)


def gram_kernel(ids, counts, blocks, sample, low, own, high, grams, compact, wide, sems):
    box = pl.program_id(0)
    count = own.shape[0]
    slots, samples = blocks.shape[1], sample.shape[2]
    half = samples // 2

    @pl.when(box == 0)
    def _():
        copies = [
            pltpu.make_async_copy(part, wide.at[pl.ds(place * count, count)], sems.at[place])
            for place, part in enumerate((low, own, high))
        ]
        for copy in copies:
            copy.start()
        for copy in copies:
            copy.wait()

    for part in range(blocks.shape[0]):
        here = box * blocks.shape[0] + part
        total = jnp.zeros(sample.shape[1:], jnp.float32)
        for slot in range(slots):
            keep = (slot < counts[here]).astype(jnp.float32).astype(jnp.bfloat16)
            picked = wide[ids[here * slots + slot]] * keep
            total += jnp.dot(blocks[part, slot], picked, preferred_element_type=jnp.float32)
        far = sample[part].astype(jnp.float32) - total
        doubled = far + pltpu.roll(far, half, 1)
        compact[part] = doubled
        random = wide[count + here].astype(jnp.float32)
        flipped = doubled.T[:half]
        grams[part] = exact_dot(flipped, jnp.concatenate([doubled, random], axis=1))


def gram_call(ids, counts, blocks, sample, low, own, high):
    count, rows, samples = sample.shape
    slots = blocks.shape[1]
    half = samples // 2
    together = 2 if count % 2 == 0 else 1
    anywhere = pl.BlockSpec(memory_space=pl.ANY)
    return pl.pallas_call(
        gram_kernel,
        grid_spec=pltpu.PrefetchScalarGridSpec(
            num_scalar_prefetch=2,
            grid=(count // together,),
            in_specs=[
                pl.BlockSpec((together, slots, rows, rows), lambda b, *_: (b, 0, 0, 0)),
                pl.BlockSpec((together, rows, samples), lambda b, *_: (b, 0, 0)),
                anywhere,
                anywhere,
                anywhere,
            ],
            out_specs=[
                pl.BlockSpec((together, half, 2 * samples), lambda b, *_: (b, 0, 0)),
                pl.BlockSpec((together, rows, samples), lambda b, *_: (b, 0, 0)),
            ],
            scratch_shapes=[
                pltpu.VMEM((3 * count, rows, samples), jnp.bfloat16),
                pltpu.SemaphoreType.DMA((3,)),
            ],
        ),
        out_shape=[
            jax.ShapeDtypeStruct((count, half, 2 * samples), jnp.float32),
            jax.ShapeDtypeStruct((count, rows, samples), jnp.float32),
        ],
        name="gram",
    )(ids, counts, blocks, sample, low, own, high)


def eliminate(nodes, low_k, high_k, half, work, uppers, with_upper):
    samples = 2 * half
    lanes = lax.broadcasted_iota(jnp.int32, (1, samples), 1)

    rows = lax.broadcasted_iota(jnp.int32, (half, samples), 0)
    group = 4

    def step(k, carry):
        at_k = lanes == k
        kept = (lanes >= k) & (lanes < half)
        row_k = rows == k
        pivots = {node: work[node, pl.ds(k, 1), :] for node in nodes}
        picked = {
            node: jnp.sum(jnp.where(at_k, pivots[node], 0.0), axis=1, keepdims=True)
            for node in nodes
        }
        scaled = {node: pivots[node] / picked[node] for node in nodes}
        for node, place in with_upper.items():
            uppers[place, pl.ds(k, 1), :] = jnp.where(
                kept, pivots[node] * lax.rsqrt(picked[node]), 0.0
            )
        for first in range(0, len(nodes), group):
            members = nodes[first : first + group]
            matrices = [work[node] for node in members]
            columns = [
                jnp.sum(jnp.where(at_k, matrix, 0.0), axis=1, keepdims=True)
                for matrix in matrices
            ]
            for node, matrix, column in zip(members, matrices, columns):
                work[node] = jnp.where(row_k, scaled[node], matrix - column * scaled[node])
        return carry

    lax.fori_loop(low_k, high_k, step, 0)


def start_matrix(gram, half):
    samples = 2 * half
    rows = lax.broadcasted_iota(jnp.int32, (half, samples), 0)
    lanes = lax.broadcasted_iota(jnp.int32, (half, samples), 1)
    return jnp.where(lanes < half, gram, (lanes - half == rows).astype(jnp.float32))


def solved(work, node, moment):
    blank = jnp.zeros_like(moment)
    answer = exact_dot(work[node], jnp.concatenate([blank, moment], axis=0))
    return jnp.concatenate([answer, blank], axis=0)


def tree_kernel(
    spread, grams, compact, leaf_out, level_out, work, moments, uppers, sums, arrived, sent, landed
):
    count = grams.shape[0]
    half, samples = grams.shape[1], grams.shape[2] // 2
    depth = count.bit_length() - 1
    me = lax.axis_index("boxes")
    bits = [lax.rem(lax.div(me, 1 << step), 2) for step in range(spread)]
    partners = [me + (1 - 2 * bit) * (1 << step) for step, bit in enumerate(bits)]
    barrier = pltpu.get_barrier_semaphore()
    for partner in partners:
        pl.semaphore_signal(
            barrier, inc=1, device_id=(partner,), device_id_type=pl.DeviceIdType.MESH
        )
    summed = grams[0]
    for leaf in range(1, count):
        summed = summed + grams[leaf]
    sums[0] = summed

    def exchange(step):
        return pltpu.make_async_remote_copy(
            src_ref=sums.at[step],
            dst_ref=arrived.at[step],
            send_sem=sent.at[step],
            recv_sem=landed.at[step],
            device_id=(partners[step],),
            device_id_type=pl.DeviceIdType.MESH,
        )

    pl.semaphore_wait(barrier, spread)
    copies = [exchange(step) for step in range(spread)]
    copies[0].start()
    for node in range(count):
        work[node] = start_matrix(grams[node, :, :samples], half)
    place = 0
    for height in range(1, depth + 1):
        for side in range(1 if height == depth else 2):
            first = side * 2**height
            part = grams[first]
            for leaf in range(first + 1, first + 2**height):
                part = part + grams[leaf]
            work[count + place] = start_matrix(part[:, :samples], half)
            moments[place] = part[:, samples:]
            place += 1
    below = count + place
    with_upper = {0: 0, 1: 1}
    for node in range(place):
        with_upper[count + node] = 2 + node
    own = 1 + place
    nodes = list(range(below))
    for step in range(spread):
        eliminate(
            nodes, half * step // spread, half * (step + 1) // spread, half, work, uppers, with_upper
        )
        copies[step].wait()
        sums[step + 1] = sums[step] + arrived[step]
        if step + 1 < spread:
            copies[step + 1].start()
    for step in range(spread):
        work[below + 2 * step] = start_matrix(arrived[step, :, :samples], half)
        work[below + 2 * step + 1] = start_matrix(sums[step + 1, :, :samples], half)
    nodes = list(range(below, below + 2 * spread))
    later = {node: own + 1 + node - below for node in nodes[:-1]}
    eliminate(nodes, 0, half, half, work, uppers, later)
    for leaf in range(count):
        answer = solved(work, leaf, grams[leaf, :, samples:])
        leaf_out[leaf] = exact_dot(compact[leaf], answer).astype(leaf_out.dtype)
    for height in range(1, depth + 1):
        place = 2 * (height - 1)
        answer = solved(work, count + place, moments[place])
        stacked = jnp.concatenate([uppers[place], uppers[place + 1]], axis=0)
        level_out[0, height - 1] = exact_dot(stacked, answer).astype(level_out.dtype)
    for step in range(spread):
        mine, other = uppers[own + 2 * step], uppers[own + 2 * step + 1]
        odd = bits[step] == 1
        stacked = jnp.concatenate(
            [jnp.where(odd, other, mine), jnp.where(odd, mine, other)], axis=0
        )
        answer = solved(work, below + 2 * step + 1, sums[step + 1, :, samples:])
        level_out[0, depth + step] = exact_dot(stacked, answer).astype(level_out.dtype)


def tree_call(grams, compact, spread):
    count, half, double = grams.shape
    samples = double // 2
    depth = count.bit_length() - 1
    extra = 2 * depth - 1
    return pl.pallas_call(
        functools.partial(tree_kernel, spread),
        in_specs=[pl.BlockSpec(memory_space=pltpu.VMEM)] * 2,
        out_specs=[pl.BlockSpec(memory_space=pltpu.VMEM)] * 2,
        out_shape=[
            jax.ShapeDtypeStruct(compact.shape, jnp.bfloat16),
            jax.ShapeDtypeStruct((1, depth + spread, samples, samples), jnp.bfloat16),
        ],
        scratch_shapes=[
            pltpu.VMEM((count + extra + 2 * spread, half, samples), jnp.float32),
            pltpu.VMEM((extra, half, samples), jnp.float32),
            pltpu.VMEM((2 + extra + 2 * spread - 1, half, samples), jnp.float32),
            pltpu.VMEM((spread + 1, half, double), jnp.float32),
            pltpu.VMEM((spread, half, double), jnp.float32),
            pltpu.SemaphoreType.DMA((spread,)),
            pltpu.SemaphoreType.DMA((spread,)),
        ],
        compiler_params=pltpu.CompilerParams(collective_id=0, has_side_effects=True),
        name="tree",
    )(grams, compact)


def per_device(random_block, sample_block, near_blocks, near_index, near_count):
    count = random_block.shape[0]
    device = lax.axis_index("boxes")
    size = lax.axis_size("boxes")
    forward = [(i, i + 1) for i in range(size - 1)]
    backward = [(target, source) for source, target in forward]
    low = lax.ppermute(random_block, "boxes", forward)
    high = lax.ppermute(random_block, "boxes", backward)
    ids = jnp.clip(near_index - device * count + count, 0, 3 * count - 1).reshape(-1)
    grams, compact = gram_call(
        ids, near_count, near_blocks, sample_block, low, random_block, high
    )
    return tuple(tree_call(grams, compact, size.bit_length() - 1))


def solution(mesh):
    return jax.shard_map(
        per_device,
        mesh=mesh,
        in_specs=(
            P("boxes", None, None),
            P("boxes", None, None),
            P("boxes", None, None, None),
            P("boxes", None),
            P("boxes"),
        ),
        out_specs=(P("boxes", None, None), P("boxes", None, None, None)),
        check_vma=False,
    )
```

```python
import functools

import jax
import jax.numpy as jnp
from jax import lax
from jax.experimental import pallas as pl
from jax.experimental.pallas import tpu as pltpu
from jax.sharding import PartitionSpec as P

exact_mode = lax.Precision.HIGHEST


def exact_dot(a, b):
    return jnp.dot(a, b, precision=exact_mode, preferred_element_type=jnp.float32)


def gram_kernel(ids, counts, blocks, sample, low, own, high, grams, compact, wide, sems):
    box = pl.program_id(0)
    count = own.shape[0]
    slots, samples = blocks.shape[1], sample.shape[2]
    half = samples // 2

    @pl.when(box == 0)
    def _():
        copies = [
            pltpu.make_async_copy(part, wide.at[pl.ds(place * count, count)], sems.at[place])
            for place, part in enumerate((low, own, high))
        ]
        for copy in copies:
            copy.start()
        for copy in copies:
            copy.wait()

    for part in range(blocks.shape[0]):
        here = box * blocks.shape[0] + part
        total = jnp.zeros(sample.shape[1:], jnp.float32)
        for slot in range(slots):
            keep = (slot < counts[here]).astype(jnp.float32).astype(jnp.bfloat16)
            picked = wide[ids[here * slots + slot]] * keep
            total += jnp.dot(blocks[part, slot], picked, preferred_element_type=jnp.float32)
        far = sample[part].astype(jnp.float32) - total
        doubled = far + pltpu.roll(far, half, 1)
        compact[part] = doubled
        random = wide[count + here].astype(jnp.float32)
        flipped = doubled.T[:half]
        grams[part] = exact_dot(flipped, jnp.concatenate([doubled, random], axis=1))


def gram_call(ids, counts, blocks, sample, low, own, high):
    count, rows, samples = sample.shape
    slots = blocks.shape[1]
    half = samples // 2
    together = 4 if count % 4 == 0 else 1
    anywhere = pl.BlockSpec(memory_space=pl.ANY)
    return pl.pallas_call(
        gram_kernel,
        grid_spec=pltpu.PrefetchScalarGridSpec(
            num_scalar_prefetch=2,
            grid=(count // together,),
            in_specs=[
                pl.BlockSpec((together, slots, rows, rows), lambda b, *_: (b, 0, 0, 0)),
                pl.BlockSpec((together, rows, samples), lambda b, *_: (b, 0, 0)),
                anywhere,
                anywhere,
                anywhere,
            ],
            out_specs=[
                pl.BlockSpec((together, half, 2 * samples), lambda b, *_: (b, 0, 0)),
                pl.BlockSpec((together, rows, samples), lambda b, *_: (b, 0, 0)),
            ],
            scratch_shapes=[
                pltpu.VMEM((3 * count, rows, samples), jnp.bfloat16),
                pltpu.SemaphoreType.DMA((3,)),
            ],
        ),
        out_shape=[
            jax.ShapeDtypeStruct((count, half, 2 * samples), jnp.float32),
            jax.ShapeDtypeStruct((count, rows, samples), jnp.float32),
        ],
        name="gram",
    )(ids, counts, blocks, sample, low, own, high)


def eliminate(nodes, low_k, high_k, half, work, uppers, with_upper):
    samples = 2 * half
    lanes = lax.broadcasted_iota(jnp.int32, (1, samples), 1)

    rows = lax.broadcasted_iota(jnp.int32, (half, samples), 0)
    group = 4

    def step(k, carry):
        at_k = lanes == k
        kept = (lanes >= k) & (lanes < half)
        row_k = rows == k
        pivots = {node: work[node, pl.ds(k, 1), :] for node in nodes}
        picked = {
            node: jnp.sum(jnp.where(at_k, pivots[node], 0.0), axis=1, keepdims=True)
            for node in nodes
        }
        scaled = {node: pivots[node] / picked[node] for node in nodes}
        for node, place in with_upper.items():
            uppers[place, pl.ds(k, 1), :] = jnp.where(
                kept, pivots[node] * lax.rsqrt(picked[node]), 0.0
            )
        for first in range(0, len(nodes), group):
            members = nodes[first : first + group]
            matrices = [work[node] for node in members]
            columns = [
                jnp.sum(jnp.where(at_k, matrix, 0.0), axis=1, keepdims=True)
                for matrix in matrices
            ]
            for node, matrix, column in zip(members, matrices, columns):
                work[node] = jnp.where(row_k, scaled[node], matrix - column * scaled[node])
        return carry

    lax.fori_loop(low_k, high_k, step, 0)


def start_matrix(gram, half):
    samples = 2 * half
    rows = lax.broadcasted_iota(jnp.int32, (half, samples), 0)
    lanes = lax.broadcasted_iota(jnp.int32, (half, samples), 1)
    return jnp.where(lanes < half, gram, (lanes - half == rows).astype(jnp.float32))


def solved(work, node, moment):
    blank = jnp.zeros_like(moment)
    answer = exact_dot(work[node], jnp.concatenate([blank, moment], axis=0))
    return jnp.concatenate([answer, blank], axis=0)


def tree_kernel(
    spread, grams, compact, leaf_out, level_out, work, moments, uppers, sums, arrived, sent, landed
):
    count = grams.shape[0]
    half, samples = grams.shape[1], grams.shape[2] // 2
    depth = count.bit_length() - 1
    me = lax.axis_index("boxes")
    bits = [lax.rem(lax.div(me, 1 << step), 2) for step in range(spread)]
    partners = [me + (1 - 2 * bit) * (1 << step) for step, bit in enumerate(bits)]
    barrier = pltpu.get_barrier_semaphore()
    for partner in partners:
        pl.semaphore_signal(
            barrier, inc=1, device_id=(partner,), device_id_type=pl.DeviceIdType.MESH
        )
    summed = grams[0]
    for leaf in range(1, count):
        summed = summed + grams[leaf]
    sums[0] = summed

    def exchange(step):
        return pltpu.make_async_remote_copy(
            src_ref=sums.at[step],
            dst_ref=arrived.at[step],
            send_sem=sent.at[step],
            recv_sem=landed.at[step],
            device_id=(partners[step],),
            device_id_type=pl.DeviceIdType.MESH,
        )

    pl.semaphore_wait(barrier, spread)
    copies = [exchange(step) for step in range(spread)]
    copies[0].start()
    for node in range(count):
        work[node] = start_matrix(grams[node, :, :samples], half)
    place = 0
    for height in range(1, depth + 1):
        for side in range(1 if height == depth else 2):
            first = side * 2**height
            part = grams[first]
            for leaf in range(first + 1, first + 2**height):
                part = part + grams[leaf]
            work[count + place] = start_matrix(part[:, :samples], half)
            moments[place] = part[:, samples:]
            place += 1
    below = count + place
    with_upper = {0: 0, 1: 1}
    for node in range(place):
        with_upper[count + node] = 2 + node
    own = 1 + place
    nodes = list(range(below))
    for step in range(spread):
        eliminate(
            nodes, half * step // spread, half * (step + 1) // spread, half, work, uppers, with_upper
        )
        copies[step].wait()
        sums[step + 1] = sums[step] + arrived[step]
        if step + 1 < spread:
            copies[step + 1].start()
    for step in range(spread):
        work[below + 2 * step] = start_matrix(arrived[step, :, :samples], half)
        work[below + 2 * step + 1] = start_matrix(sums[step + 1, :, :samples], half)
    nodes = list(range(below, below + 2 * spread))
    later = {node: own + 1 + node - below for node in nodes[:-1]}
    eliminate(nodes, 0, half, half, work, uppers, later)
    for leaf in range(count):
        answer = solved(work, leaf, grams[leaf, :, samples:])
        leaf_out[leaf] = exact_dot(compact[leaf], answer).astype(leaf_out.dtype)
    for height in range(1, depth + 1):
        place = 2 * (height - 1)
        answer = solved(work, count + place, moments[place])
        stacked = jnp.concatenate([uppers[place], uppers[place + 1]], axis=0)
        level_out[0, height - 1] = exact_dot(stacked, answer).astype(level_out.dtype)
    for step in range(spread):
        mine, other = uppers[own + 2 * step], uppers[own + 2 * step + 1]
        odd = bits[step] == 1
        stacked = jnp.concatenate(
            [jnp.where(odd, other, mine), jnp.where(odd, mine, other)], axis=0
        )
        answer = solved(work, below + 2 * step + 1, sums[step + 1, :, samples:])
        level_out[0, depth + step] = exact_dot(stacked, answer).astype(level_out.dtype)


def tree_call(grams, compact, spread):
    count, half, double = grams.shape
    samples = double // 2
    depth = count.bit_length() - 1
    extra = 2 * depth - 1
    return pl.pallas_call(
        functools.partial(tree_kernel, spread),
        in_specs=[pl.BlockSpec(memory_space=pltpu.VMEM)] * 2,
        out_specs=[pl.BlockSpec(memory_space=pltpu.VMEM)] * 2,
        out_shape=[
            jax.ShapeDtypeStruct(compact.shape, jnp.bfloat16),
            jax.ShapeDtypeStruct((1, depth + spread, samples, samples), jnp.bfloat16),
        ],
        scratch_shapes=[
            pltpu.VMEM((count + extra + 2 * spread, half, samples), jnp.float32),
            pltpu.VMEM((extra, half, samples), jnp.float32),
            pltpu.VMEM((2 + extra + 2 * spread - 1, half, samples), jnp.float32),
            pltpu.VMEM((spread + 1, half, double), jnp.float32),
            pltpu.VMEM((spread, half, double), jnp.float32),
            pltpu.SemaphoreType.DMA((spread,)),
            pltpu.SemaphoreType.DMA((spread,)),
        ],
        compiler_params=pltpu.CompilerParams(collective_id=0, has_side_effects=True),
        name="tree",
    )(grams, compact)


def per_device(random_block, sample_block, near_blocks, near_index, near_count):
    count = random_block.shape[0]
    device = lax.axis_index("boxes")
    size = lax.axis_size("boxes")
    forward = [(i, i + 1) for i in range(size - 1)]
    backward = [(target, source) for source, target in forward]
    low = lax.ppermute(random_block, "boxes", forward)
    high = lax.ppermute(random_block, "boxes", backward)
    ids = jnp.clip(near_index - device * count + count, 0, 3 * count - 1).reshape(-1)
    grams, compact = gram_call(
        ids, near_count, near_blocks, sample_block, low, random_block, high
    )
    return tuple(tree_call(grams, compact, size.bit_length() - 1))


def solution(mesh):
    return jax.shard_map(
        per_device,
        mesh=mesh,
        in_specs=(
            P("boxes", None, None),
            P("boxes", None, None),
            P("boxes", None, None, None),
            P("boxes", None),
            P("boxes"),
        ),
        out_specs=(P("boxes", None, None), P("boxes", None, None, None)),
        check_vma=False,
    )
```
